32 devices in a mesh: row: 8 (over y, x, core), col: 4 (over z).
Axes of the slice: x: 2, y: 2, z: 4, core: 2. Of those that a mesh axis runs over, the one named last changes fastest.
Arguments:
- hidden_in: bfloat16 [1152, 2048], P('col', 'row'), may hold values from -21 to 21
- state: float32 [128, 2048, 1152], P('col', 'row'), may hold values from -4 to 4
- attn_norm_gain: bfloat16 [2048], replicated, may hold values from 0.099609375 to 1.8984375
- w_query: bfloat16 [2048, 2048], P(None, 'row'), may hold values from -0.125 to 0.125
- w_key: bfloat16 [2048, 2048], P(None, 'row'), may hold values from -0.125 to 0.125
- w_value: bfloat16 [2048, 2048], P(None, 'row'), may hold values from -0.125 to 0.125
- w_gate: bfloat16 [2048, 2048], P(None, 'row'), may hold values from -0.125 to 0.125
- w_decay: bfloat16 [2048, 16], replicated, may hold values from -0.125 to 0.125
- w_beta: bfloat16 [2048, 16], replicated, may hold values from -0.125 to 0.125
- decay_log: float32 [16], replicated, may hold values from -3 to 1.5
- decay_bias: float32 [16], replicated, may hold values from -2 to 1
- head_gain: float32 [128], replicated, may hold values from 0.1 to 1.9
- w_out: bfloat16 [2048, 2048], P('row'), may hold values from -0.125 to 0.125
- final_gain: bfloat16 [2048], P('row'), may hold values from 0.099609375 to 1.8984375
- lm_weight: bfloat16 [2048, 20480], P(None, ('row', 'col')), may hold values from -0.28726213 to 0.28726213
- token_ids: int32 [1152], replicated, may hold values from 0 to 20479
- ref_logprob: float32 [1152], replicated, may hold values from -16 to -6
Outputs:
- new_state: float32 [128, 2048, 1152], P('col', 'row')
- logprob: float32 [1152], replicated
- entropy: float32 [1152], replicated
- kl: float32 [1152], replicated
The draws below stay inside these ranges and needn't reach their ends.
All inputs are finite; a program needn't handle non-finite values.
Results may differ from the reference program's by a relative error of at most 0.0014.
The reference program's roundings to bfloat16 on the way (of `normed`, `mixed_heads` and `final`) count: a program that leaves them out, or rounds other values in their place, can miss the bound.
Values may be sent and summed in bfloat16 or wider, within the bound.
A program may use at most 128 MiB of HBM per device.

```python
import jax
import jax.numpy as jnp
from jax import lax

D = 2048
HEADS = 16
DK = 128
DV = 128
VOCAB_DEV = 640
BATCH = 1152
VOCAB = 20480


def shared_sign(key):
    flips = jax.random.bernoulli(jax.random.fold_in(key, 101), 0.5, (D,))
    return jnp.where(flips, 1.0, -1.0).astype(jnp.float32)


def aligned_rows(key):
    level = jax.random.randint(jax.random.fold_in(key, 102), (BATCH,), 0, 3)
    chosen_rows = jnp.arange(BATCH, dtype=jnp.int32) % 5 == 0
    strength = 1.5 * jnp.exp2(level.astype(jnp.float32))
    return jnp.where(chosen_rows, strength, 0.0)


def draw_hidden_in(key, part):
    column_scale = 1.0 + 2.0 * jnp.arange(D, dtype=jnp.float32) / D
    strength = aligned_rows(key)
    base = jnp.clip(jax.random.normal(jax.random.fold_in(key, 3), (BATCH, D), jnp.float32), -4.0, 4.0)
    spread = base * column_scale[None, :]
    aligned = strength[:, None] * shared_sign(key)[None, :] + base
    values = jnp.where(strength[:, None] > 0.0, aligned, spread)
    return values.astype(jnp.bfloat16)


def draw_lm_weight(key, part):
    column_scale = 1.0 + 2.0 * jnp.arange(VOCAB, dtype=jnp.float32) / VOCAB
    base = jnp.clip(jax.random.normal(jax.random.fold_in(key, 6), (D, VOCAB), jnp.float32), -4.0, 4.0)
    base = base * column_scale[None, :] / jnp.sqrt(jnp.float32(D))
    chosen = jax.random.randint(jax.random.fold_in(key, 5), (4,), 0, VOCAB - 1)
    heights = (280.0 - 30.0 * jnp.arange(4, dtype=jnp.float32)) / jnp.float32(D)
    strength = jnp.zeros((VOCAB,), jnp.float32)
    strength = strength.at[chosen + 1].set(heights - 2.0 / jnp.float32(D))
    strength = strength.at[chosen].set(heights)
    values = jnp.where(strength[None, :] > 0.0, shared_sign(key)[:, None] * strength[None, :], base)
    return values.astype(jnp.bfloat16)


def plant(values, own_key, least, top_value):
    index_at = [jax.random.randint(jax.random.fold_in(own_key, axis), (), 0, length) for axis, length in enumerate(values.shape)]
    longest = values.shape.index(max(values.shape))
    next_to = index_at[:longest] + [(index_at[longest] + 1) % values.shape[longest]] + index_at[longest + 1:]
    return values.at[tuple(index_at)].set(least).at[tuple(next_to)].set(top_value)


def steps_of(key, shape, pieces, low, largest):
    factor_of, own = 1.0, jax.random.fold_in(key, 6)
    for dim, shards_of in pieces:
        draws = jnp.exp(jax.random.uniform(jax.random.fold_in(own, dim), (shards_of,), jnp.float32, low / len(pieces), largest / len(pieces)))
        factor_of = factor_of * jnp.repeat(draws, shape[dim] // shards_of).reshape([-1 if axis == dim else 1 for axis in range(len(shape))])
    return factor_of


def bell_draw(key, dims, scale, limit, cuts=(), kind=jnp.bfloat16):
    values = jax.random.normal(key, dims, jnp.float32) * scale
    if len(cuts) > 0:
        values = steps_of(key, dims, cuts, -0.22, 0.18) * values
    return jnp.clip(values, min=-limit, max=limit).astype(kind)


def setup_inputs(seed: int = 0) -> dict:
    keys = jax.random.split(jax.random.key(seed), 18)
    return {
        "hidden_in": draw_hidden_in(jax.random.fold_in(keys[17], 71), 0),
        "state": bell_draw(keys[1], (DK, HEADS * DV, BATCH), 0.5, 4.0, ((0, 4), (1, 8)), jnp.float32),
        "attn_norm_gain": jnp.clip(1.0 + 0.18 * jax.random.normal(keys[2], (D,), jnp.float32), 0.099609375, 1.8984375).astype(jnp.bfloat16),
        "w_query": bell_draw(keys[3], (D, HEADS * DK), D ** -0.5, 0.125, ((1, 8),)),
        "w_key": bell_draw(keys[4], (D, HEADS * DK), D ** -0.5, 0.125, ((1, 8),)),
        "w_value": bell_draw(keys[5], (D, HEADS * DV), D ** -0.5, 0.125, ((1, 8),)),
        "w_gate": bell_draw(keys[6], (D, HEADS * DV), D ** -0.5, 0.125, ((1, 8),)),
        "w_decay": bell_draw(keys[7], (D, HEADS), D ** -0.5, 0.125),
        "w_beta": bell_draw(keys[8], (D, HEADS), D ** -0.5, 0.125),
        "decay_log": jnp.clip(jax.random.uniform(keys[9], (HEADS,), jnp.float32, -3.0, 1.5), -3.0, 1.5),
        "decay_bias": jnp.clip(jax.random.uniform(keys[10], (HEADS,), jnp.float32, -2.0, 1.0), -2.0, 1.0),
        "head_gain": jnp.clip(1.0 + 0.18 * jax.random.normal(keys[11], (DV,), jnp.float32), 0.1, 1.9),
        "w_out": bell_draw(keys[12], (HEADS * DV, D), (HEADS * DV) ** -0.5, 0.125, ((0, 8),)),
        "final_gain": jnp.clip(1.0 + 0.18 * jax.random.normal(keys[13], (D,), jnp.float32), 0.099609375, 1.8984375).astype(jnp.bfloat16),
        "lm_weight": draw_lm_weight(jax.random.fold_in(keys[17], 71), 0),
        "token_ids": plant(jax.random.randint(keys[15], (BATCH,), 0, VOCAB), jax.random.fold_in(keys[15], 1), 0, VOCAB - 1).astype(jnp.int32),
        "ref_logprob": jnp.clip(jax.random.uniform(keys[16], (BATCH,), jnp.float32, -16.0, -6.0), -16.0, -6.0),
    }


def reference(hidden_in, state, attn_norm_gain, w_query, w_key, w_value, w_gate, w_decay, w_beta, decay_log, decay_bias, head_gain, w_out, final_gain, lm_weight, token_ids, ref_logprob):
    highest = lax.Precision.HIGHEST
    x = hidden_in.astype(jnp.float32)
    normed = (x * lax.rsqrt(lax.optimization_barrier(jnp.mean(x * x, axis=1, keepdims=True)) + 1e-06) * attn_norm_gain.astype(jnp.float32)).astype(jnp.bfloat16)
    qraw = lax.optimization_barrier(jnp.dot(normed, w_query, preferred_element_type=jnp.float32).astype(jnp.bfloat16)).astype(jnp.float32).reshape(BATCH, HEADS, DK)
    kraw = lax.optimization_barrier(jnp.dot(normed, w_key, preferred_element_type=jnp.float32).astype(jnp.bfloat16)).astype(jnp.float32).reshape(BATCH, HEADS, DK)
    query = (qraw * lax.rsqrt(lax.optimization_barrier(jnp.sum(qraw * qraw, axis=2, keepdims=True)) + 1e-06)).astype(jnp.bfloat16).astype(jnp.float32)
    key = (kraw * lax.rsqrt(lax.optimization_barrier(jnp.sum(kraw * kraw, axis=2, keepdims=True)) + 1e-06)).astype(jnp.bfloat16).astype(jnp.float32)
    value = jnp.dot(normed, w_value, preferred_element_type=jnp.float32).reshape(BATCH, HEADS, DV)
    gate = jnp.dot(normed, w_gate, preferred_element_type=jnp.float32).reshape(BATCH, HEADS, DV)
    decay_in = jnp.dot(normed, w_decay, preferred_element_type=jnp.float32)
    alpha = jnp.exp(-jnp.exp(decay_log)[None, :] * jax.nn.softplus(decay_in + decay_bias[None, :]))
    beta = jax.nn.sigmoid(jnp.dot(normed, w_beta, preferred_element_type=jnp.float32))
    alpha_t = alpha.T
    beta_t = beta.T
    tiles = state.reshape(DK, HEADS, DV, BATCH)
    recall = jnp.einsum('khvb,bhk->hvb', tiles, key, precision=highest)
    value_t = jnp.transpose(value, (1, 2, 0))
    write = beta_t[:, None, :] * (value_t - alpha_t[:, None, :] * recall)
    key_t = jnp.transpose(key, (2, 1, 0))
    updated = alpha_t[None, :, None, :] * tiles + key_t[:, :, None, :] * write[None]
    readout = jnp.einsum('khvb,bhk->hvb', updated, query, precision=highest)
    power = lax.optimization_barrier(jnp.mean(readout * readout, axis=1, keepdims=True))
    gate_t = jnp.transpose(gate, (1, 2, 0))
    mixed = readout * lax.rsqrt(power + 1e-05) * head_gain[None, :, None] * jax.nn.silu(gate_t)
    mixed_heads = jnp.transpose(mixed, (2, 0, 1)).reshape(BATCH, HEADS * DV).astype(jnp.bfloat16)
    hidden = x + jnp.dot(mixed_heads, w_out, preferred_element_type=jnp.float32)
    final = (hidden * lax.rsqrt(lax.optimization_barrier(jnp.mean(hidden * hidden, axis=1, keepdims=True)) + 1e-06) * final_gain.astype(jnp.float32)).astype(jnp.bfloat16)
    shards = VOCAB // VOCAB_DEV
    columns = jnp.arange(VOCAB_DEV, dtype=jnp.int32)

    def shard_step(index, carry):
        top, total, weighted, picked = carry
        piece = lax.dynamic_slice_in_dim(lm_weight, (index * VOCAB_DEV).astype(jnp.int32), VOCAB_DEV, 1)
        logits = jnp.dot(final, piece, preferred_element_type=jnp.float32)
        local_top = lax.optimization_barrier(jnp.max(logits, axis=1))
        new_top = jnp.maximum(top, local_top)
        shrink = jnp.exp(top - new_top)
        expo = jnp.exp(logits - new_top[:, None])
        total = total * shrink + lax.optimization_barrier(jnp.sum(expo, axis=1))
        weighted = weighted * shrink + lax.optimization_barrier(jnp.sum(expo * logits, axis=1))
        hits = columns[None, :] + (index * VOCAB_DEV).astype(jnp.int32) == token_ids[:, None]
        picked = picked + lax.optimization_barrier(jnp.sum(jnp.where(hits, logits, jnp.zeros_like(logits)), axis=1))
        return (new_top, total, weighted, picked)
    start = (jnp.full((BATCH,), -1e+30, jnp.float32), jnp.zeros((BATCH,), jnp.float32), jnp.zeros((BATCH,), jnp.float32), jnp.zeros((BATCH,), jnp.float32))
    top, total, weighted, picked = lax.fori_loop(jnp.int32(0), jnp.int32(shards), shard_step, start)
    lse = top + jnp.log(total)
    logprob = picked - lse
    entropy = lse - weighted / total
    gap = jnp.clip(ref_logprob - logprob, -20.0, 20.0)
    kl = jnp.minimum(jnp.exp(gap) - gap - 1.0, 10.0)
    new_state = updated.reshape(DK, HEADS * DV, BATCH)
    return (new_state, logprob, entropy, kl)
```

```python
import jax
import jax.numpy as jnp
from jax import lax
from jax.sharding import PartitionSpec as P

D = 2048
HEADS = 16
DK = 128
DV = 128


def partner_2(block, axis, apart):
    count = lax.axis_size(axis)
    route = []
    for low in range(count):
        high = low | 1 << apart
        if high != low and high < count:
            route += [(low, high), (high, low)]
    return lax.ppermute(block, axis, route)


def project(weight, normed):
    return lax.dot_general(
        weight, normed, (((0,), (1,)), ((), ())), preferred_element_type=jnp.float32
    )


def shift_pairs(count, step):
    return [(source, (source + step) % count) for source in range(count)]


def swap_blocks(blocks, axis):
    count = lax.axis_size(axis)
    me = lax.axis_index(axis)
    result = blocks
    for step in range(1, count):
        sent = lax.dynamic_index_in_dim(blocks, (me + step) % count, 0, keepdims=True)
        got = lax.ppermute(sent, axis, shift_pairs(count, step))
        result = lax.dynamic_update_slice_in_dim(result, got, (me - step) % count, 0)
    return result


def gather_blocks(block, axis):
    count = lax.axis_size(axis)
    me = lax.axis_index(axis)
    result = jnp.zeros((count,) + block.shape, block.dtype)
    result = lax.dynamic_update_slice_in_dim(result, block[None], me, 0)
    for step in range(1, count):
        got = lax.ppermute(block[None], axis, shift_pairs(count, step))
        result = lax.dynamic_update_slice_in_dim(result, got, (me - step) % count, 0)
    return result


def sum_blocks(blocks, axis):
    count = lax.axis_size(axis)
    me = lax.axis_index(axis)
    total = lax.dynamic_index_in_dim(blocks, me, 0, keepdims=False)
    for step in range(1, count):
        sent = lax.dynamic_index_in_dim(blocks, (me + step) % count, 0, keepdims=False)
        total = total + lax.ppermute(sent, axis, shift_pairs(count, step))
    return total


def merge_stats(stats, axis):
    every = lax.all_gather(stats, axis, axis=0, tiled=False)
    top = jnp.max(every[:, 0], axis=0)
    shrink = jnp.exp(every[:, 0] - top[None])
    return jnp.stack(
        [
            top,
            jnp.sum(every[:, 1] * shrink, axis=0),
            jnp.sum(every[:, 2] * shrink, axis=0),
            jnp.sum(every[:, 3], axis=0),
        ]
    )


def per_device(
    hidden_in,
    state,
    attn_norm_gain,
    w_query,
    w_key,
    w_value,
    w_gate,
    w_decay,
    w_beta,
    decay_log,
    decay_bias,
    head_gain,
    w_out,
    final_gain,
    lm_weight,
    token_ids,
    ref_logprob,
):
    highest = lax.Precision.HIGHEST
    row_count = lax.axis_size("row")
    col_count = lax.axis_size("col")
    row_index = lax.axis_index("row")
    col_index = lax.axis_index("col")
    group = max(1, row_count // HEADS)
    local_heads = max(1, HEADS // row_count)
    first_head = row_index // group * local_heads
    value_cols = w_value.shape[1]
    value_part = value_cols // local_heads
    block_rows = hidden_in.shape[0]
    key_rows = state.shape[0]
    batch = state.shape[2]
    vocab_dev = lm_weight.shape[1]
    packed = jnp.concatenate([hidden_in, final_gain[None, :]], axis=0)
    whole = lax.all_gather(packed, "row", axis=1, tiled=True)
    whole_rows = whole[:block_rows]
    whole_gain = whole[block_rows].astype(jnp.float32)
    xfull = whole_rows.astype(jnp.float32)
    normed = (
        xfull
        * lax.rsqrt(jnp.mean(xfull * xfull, axis=1, keepdims=True) + 1e-06)
        * attn_norm_gain.astype(jnp.float32)
    ).astype(jnp.bfloat16)
    raw_pair = jnp.stack([project(w_query, normed), project(w_key, normed)]).astype(jnp.bfloat16)
    raw_pair = lax.optimization_barrier(raw_pair)
    for level in range(group.bit_length() - 1):
        partner = partner_2(raw_pair, "row", level)
        upper = row_index >> level & 1 == 1
        raw_pair = jnp.where(
            upper,
            jnp.concatenate([partner, raw_pair], axis=1),
            jnp.concatenate([raw_pair, partner], axis=1),
        )
    pair_f = raw_pair.astype(jnp.float32).reshape(2, local_heads, DK, block_rows)
    unit_pair = (
        pair_f * lax.rsqrt(jnp.sum(pair_f * pair_f, axis=2, keepdims=True) + 1e-06)
    ).astype(jnp.bfloat16)
    key_blocks = unit_pair.reshape(2, local_heads, col_count, key_rows, block_rows)
    swapped = swap_blocks(jnp.transpose(key_blocks, (2, 0, 1, 3, 4)), "col")
    tiles_qk = jnp.transpose(swapped, (1, 2, 3, 0, 4)).reshape(2, local_heads, key_rows, batch)
    query = tiles_qk[0].astype(jnp.float32)
    key = tiles_qk[1].astype(jnp.float32)
    unit_f = unit_pair.astype(jnp.float32)
    intersection = jnp.sum(unit_f[0] * unit_f[1], axis=1)
    value_t = project(w_value, normed)
    gate_t = project(w_gate, normed)
    decay_in = lax.dynamic_slice_in_dim(project(w_decay, normed), first_head, local_heads, 0)
    beta_in = lax.dynamic_slice_in_dim(project(w_beta, normed), first_head, local_heads, 0)
    rate = jnp.exp(lax.dynamic_slice_in_dim(decay_log, first_head, local_heads, 0))
    bias = lax.dynamic_slice_in_dim(decay_bias, first_head, local_heads, 0)
    alpha_t = jnp.exp(-rate[:, None] * jax.nn.softplus(decay_in + bias[:, None]))
    beta_t = jax.nn.sigmoid(beta_in)
    tiles = state.reshape(key_rows, local_heads, value_part, batch)
    value4 = value_t.reshape(local_heads, value_part, block_rows)
    key_major = jnp.transpose(key, (1, 0, 2))
    responses = jnp.stack(
        [
            jnp.einsum("khvb,hkb->hvb", tiles, key, precision=highest),
            jnp.einsum("khvb,hkb->hvb", tiles, query, precision=highest),
        ]
    )
    responses = responses.reshape(2, local_heads, value_part, col_count, block_rows)
    recall, answer = lax.psum_scatter(jnp.transpose(responses, (3, 0, 1, 2, 4)), "col", scatter_dimension=0, tiled=False)
    write = beta_t[:, None, :] * (value4 - alpha_t[:, None, :] * recall)
    parts = gather_blocks(
        jnp.concatenate([write.reshape(value_cols, block_rows), alpha_t], axis=0), "col"
    )
    parts = jnp.transpose(parts, (1, 0, 2)).reshape(value_cols + local_heads, batch)
    write_all = parts[:value_cols].reshape(local_heads, value_part, batch)
    alpha_all = parts[value_cols:]
    updated = alpha_all[None, :, None, :] * tiles + key_major[:, :, None, :] * write_all[None]
    readout = alpha_t[:, None, :] * answer + intersection[:, None, :] * write
    power = jnp.sum(readout * readout, axis=1)
    for level in range(group.bit_length() - 1):
        power = power + partner_2(power, "row", level)
    gain_part = lax.dynamic_slice_in_dim(head_gain, row_index % group * value_part, value_part, 0)
    gate4 = gate_t.reshape(local_heads, value_part, block_rows)
    mixed = (
        readout
        * lax.rsqrt(power / DV + 1e-05)[:, None, :]
        * gain_part[None, :, None]
        * jax.nn.silu(gate4)
    )
    mixed_heads = mixed.reshape(value_cols, block_rows).astype(jnp.bfloat16)
    share = -(-block_rows // row_count)
    extra = share * row_count - block_rows
    partial = lax.dot_general(
        mixed_heads, w_out, (((0,), (0,)), ((), ())), preferred_element_type=jnp.float32
    )
    branch = lax.psum_scatter(
        jnp.pad(partial, ((0, extra), (0, 0))).reshape(row_count, share, D),
        "row",
        scatter_dimension=0,
        tiled=False,
    )
    own_rows = lax.dynamic_slice_in_dim(
        jnp.pad(whole_rows, ((0, extra), (0, 0))), row_index * share, share, 0
    )
    hidden = own_rows.astype(jnp.float32) + branch
    energy = jnp.mean(hidden * hidden, axis=1, keepdims=True)
    final = (hidden * lax.rsqrt(energy + 1e-06) * whole_gain[None, :]).astype(jnp.bfloat16)
    tall = lax.all_gather(final, ("col", "row"), axis=0, tiled=True)
    if extra:
        tall = tall.reshape(col_count, share * row_count, D)[:, :block_rows].reshape(batch, D)
    logits = jnp.dot(tall, lm_weight, preferred_element_type=jnp.float32)
    vocab_start = (row_index * col_count + col_index) * vocab_dev
    hits = jnp.arange(vocab_dev, dtype=jnp.int32)[None, :] + vocab_start == token_ids[:, None]
    local_pick = jnp.sum(jnp.where(hits, logits, jnp.zeros_like(logits)), axis=1)
    local_top = jnp.max(logits, axis=1)
    expo = jnp.exp(logits - local_top[:, None])
    local_total = jnp.sum(expo, axis=1)
    local_weighted = jnp.sum(expo * logits, axis=1)
    stats = jnp.stack([local_top, local_total, local_weighted, local_pick])
    top, total, weighted, picked = merge_stats(merge_stats(stats, "col"), "row")
    lse = top + jnp.log(total)
    logprob = picked - lse
    entropy = lse - weighted / total
    gap = jnp.clip(ref_logprob - logprob, -20.0, 20.0)
    kl = jnp.minimum(jnp.exp(gap) - gap - 1.0, 10.0)
    new_state = updated.reshape(key_rows, value_cols, batch)
    return (new_state, logprob, entropy, kl)


def solution(mesh):
    in_specs = (
        P("col", "row"),
        P("col", "row", None),
        P(),
        P(None, "row"),
        P(None, "row"),
        P(None, "row"),
        P(None, "row"),
        P(),
        P(),
        P(),
        P(),
        P(),
        P("row", None),
        P("row"),
        P(None, ("row", "col")),
        P(),
        P(),
    )
    out_specs = (P("col", "row", None), P(), P(), P())
    return jax.shard_map(
        per_device, mesh=mesh, in_specs=in_specs, out_specs=out_specs, check_vma=False
    )
```
